32 devices in a mesh: leaf: 8 (over z, y), row: 4 (over x, core).
Axes of the slice: x: 2, y: 2, z: 4, core: 2. Of those that a mesh axis runs over, the one named last changes fastest.
Arguments:
- rhs_blocks: float32 [7, 1024, 256], P(None, 'leaf'), may hold values from -6 to 6
- diag_inverse: float32 [7, 1024, 1024], P(None, 'leaf', 'row'), may hold values from -0.1875 to 0.1875
- lower_blocks: float32 [6, 1024, 1024], P(None, 'leaf', 'row'), may hold values from -0.09375 to 0.09375
- update_rows: int32 [6, 1024], P(None, 'leaf'), may hold values from 512 to 895, as said below
Outputs:
- solution: float32 [7, 1024, 256], P(None, 'leaf')
The draws below stay inside these ranges and needn't reach their ends.
Inputs may be any that keep to these rules, and one draw needn't show every extreme that they name: update_rows[s, m] = a * 128 + c names column i * 128 + c of an ancestor a of supernode s, where i = m // 128; the 128 entries of one supernode with the same i are distinct.
All inputs are finite; a program needn't handle non-finite values.
Results may differ from the reference program's by a relative error of at most 0.0001.
Values sent between devices are 32-bit elements; how exact they have to be, the bound alone decides.
No kernel may reach another device: no remote copies, remote signals or barrier semaphores. Data moves between devices by JAX's collectives and lax.ppermute only.
A program may use at most 64 MiB of HBM per device.

```python
import jax
import jax.numpy as jnp
from jax import lax

RHS = 256
PANEL = 128
LEVELS = 3
NODES = 7
SEP = 1024


def node_place(supernode):
    for depth_level in range(LEVELS):
        first_node = 2 ** LEVELS - 2 ** (depth_level + 1)
        if first_node <= supernode < first_node + 2 ** depth_level:
            return (depth_level, supernode - first_node)
    return (0, 0)


def ancestry(supernode):
    depth_level, within = node_place(supernode)
    result_list = []
    for upward in range(depth_level):
        depth_level = depth_level - 1
        within = within // 2
        result_list.append(2 ** LEVELS - 2 ** (depth_level + 1) + within)
    return result_list


def draw_update_rows(key, part):
    leaf_count = SEP // PANEL
    row_lists = []
    for supernode in range(NODES - 1):
        parents = ancestry(supernode)
        candidates = jnp.concatenate([jnp.arange(parent * PANEL, (parent + 1) * PANEL, dtype=jnp.int32) for parent in parents])
        parent_columns = jnp.arange(parents[0] * PANEL, (parents[0] + 1) * PANEL, dtype=jnp.int32)
        subkeys = jax.random.split(jax.random.fold_in(key, supernode), leaf_count)
        first_block = jax.random.permutation(subkeys[0], parent_columns)[None, :]
        other_blocks = jax.vmap(lambda subkey: jax.random.permutation(subkey, candidates)[:PANEL])(subkeys[1:])
        selected = jnp.concatenate([first_block, other_blocks], axis=0)
        row_lists.append(selected.reshape(-1))
    return jnp.stack(row_lists).astype(jnp.int32)


def steps_of(stream_key, shape, shards, smallest, high):
    level = 1.0
    for position, shards_of in shards:
        steps = jax.random.uniform(jax.random.fold_in(jax.random.fold_in(stream_key, 6), position), (shards_of,), jnp.float32, smallest / len(shards), high / len(shards))
        level = level * jnp.repeat(jnp.exp(steps), shape[position] // shards_of).reshape((-1,) + (1,) * (len(shape) - 1 - position))
    return level


def normal_values(own_key, extent, width, reach, shards=(), kind=jnp.bfloat16):
    gain = steps_of(own_key, extent, shards, -0.22, 0.18) if shards else 1.0
    drawn = jax.random.normal(own_key, extent, jnp.float32) * width * gain
    return jnp.minimum(jnp.maximum(drawn, -reach), reach).astype(kind)


def setup_inputs(seed: int = 0) -> dict:
    key_list = jax.random.split(jax.random.key(seed), 5)
    rhs_blocks = normal_values(key_list[0], (NODES, SEP, RHS), 1.0, 6.0, ((1, 8),), jnp.float32)
    diag_inverse = normal_values(key_list[1], (NODES, SEP, SEP), SEP ** -0.5, 0.1875, ((1, 8), (2, 4)), jnp.float32)
    lower_blocks = normal_values(key_list[2], (NODES - 1, SEP, SEP), (4 * SEP) ** -0.5, 0.09375, ((1, 8), (2, 4)), jnp.float32)
    update_rows = draw_update_rows(jax.random.fold_in(key_list[4], 71), 0)
    return dict(rhs_blocks=rhs_blocks, diag_inverse=diag_inverse, lower_blocks=lower_blocks, update_rows=update_rows)


def level_offset(depth_level):
    return 2 ** LEVELS - 2 ** (depth_level + 1)


def reference(rhs_blocks, diag_inverse, lower_blocks, update_rows):
    total_rows = NODES * SEP
    leaf_block = jnp.arange(SEP, dtype=jnp.int32) // PANEL
    targets = (update_rows // PANEL) * SEP + leaf_block[None, :] * PANEL + update_rows % PANEL
    current = rhs_blocks.reshape(total_rows, RHS)
    forward_list = []
    for depth_level in range(LEVELS - 1, -1, -1):
        first_node = level_offset(depth_level)
        node_count = 2 ** depth_level
        stop_node = first_node + node_count
        gathered = current[first_node * SEP:stop_node * SEP].reshape(node_count, SEP, RHS)
        forward = jnp.einsum("scr,sct->srt", diag_inverse[first_node:stop_node], gathered,
                             precision=lax.Precision.HIGHEST)
        forward_list.append(forward)
        if depth_level > 0:
            update = jnp.einsum("smr,srt->smt", lower_blocks[first_node:stop_node], forward,
                                precision=lax.Precision.HIGHEST)
            current = current.at[targets[first_node:stop_node].reshape(-1)].add(-update.reshape(-1, RHS))
    by_level = forward_list[::-1]
    answer = jnp.zeros((total_rows, RHS), jnp.float32)
    for depth_level in range(LEVELS):
        first_node = level_offset(depth_level)
        node_count = 2 ** depth_level
        stop_node = first_node + node_count
        residual = by_level[depth_level]
        if depth_level > 0:
            known = answer[targets[first_node:stop_node].reshape(-1)].reshape(node_count, SEP, RHS)
            residual = residual - jnp.einsum("smr,smt->srt", lower_blocks[first_node:stop_node], known,
                                             precision=lax.Precision.HIGHEST)
        backward = jnp.einsum("scr,srt->sct", diag_inverse[first_node:stop_node], residual,
                              precision=lax.Precision.HIGHEST)
        answer = answer.at[first_node * SEP:stop_node * SEP].set(backward.reshape(-1, RHS))
    return answer.reshape(NODES, SEP, RHS)
```

```python
import jax
import jax.numpy as jnp
from jax import lax
from jax.sharding import PartitionSpec as P

AXES = ("leaf", "row")
PRECISION = lax.Precision.HIGHEST


def dot(left, right, dims):
    return lax.dot_general(
        left, right, (dims, ((), ())), precision=PRECISION, preferred_element_type=jnp.float32
    )


def local(rhs_blocks, diag_inverse, lower_blocks, update_rows):
    leaf_count = lax.axis_size("leaf")
    row_count = lax.axis_size("row")
    node_total, panel, width = rhs_blocks.shape
    piece = diag_inverse.shape[2]
    levels = (node_total + 1).bit_length() - 1
    planes = 2 ** (levels - 1)
    inner = leaf_count // planes
    cross = row_count // 2
    half = width // 2
    group = half // planes
    first = [2**levels - 2 ** (d + 1) for d in range(levels)]
    shift = [levels - 1 - d for d in range(levels)]

    leaf_index = lax.axis_index("leaf")
    plane = leaf_index // inner
    core = lax.axis_index("row") % 2

    def move(x, plane_mask=0, inner_mask=0, cross_mask=0, core_mask=0):
        pairs = []
        for leaf in range(leaf_count):
            for row in range(row_count):
                other_leaf = leaf ^ (plane_mask * inner + inner_mask)
                other_row = row ^ (cross_mask * 2 + core_mask)
                pairs.append((leaf * row_count + row, other_leaf * row_count + other_row))
        return lax.ppermute(x, AXES, pairs)

    def inner_sum(x):
        mask = 1
        while mask < inner:
            x = x + move(x, inner_mask=mask)
            mask *= 2
        return x

    def cross_sum(x, plane_mask=0):
        parts = [
            move(x, plane_mask=plane_mask, cross_mask=m) if m or plane_mask else x
            for m in range(cross)
        ]
        while len(parts) > 1:
            parts = [parts[i] + parts[i + 1] for i in range(0, len(parts), 2)]
        return parts[0]

    def reverse(mask):
        return sum(((mask >> b) & 1) << (levels - 2 - b) for b in range(levels - 1))

    def reorder(x, mask):
        parts = [x[:, (o ^ mask) * panel : ((o ^ mask) + 1) * panel] for o in range(planes)]
        return jnp.concatenate(parts, axis=1)

    def regroup(x, mask):
        if mask == 0:
            return x
        count = x.shape[0] // group
        g = reverse(mask)
        return jnp.concatenate(
            [x[(i ^ g) * group : ((i ^ g) + 1) * group] for i in range(count)], axis=0
        )

    def pick(array, index):
        return lax.dynamic_index_in_dim(array, index, 0, keepdims=False)

    def gather_node(blocks, depth):
        parts = []
        for o in range(planes):
            node = first[depth] + ((plane ^ o) >> shift[depth])
            block = pick(blocks, node)
            parts.append(block if o == 0 else move(block, plane_mask=o))
        own = jnp.concatenate(parts, axis=0)
        return own

    def pair_core(own):
        return jnp.concatenate([own, move(own, core_mask=1)], axis=1)

    flipped = jnp.swapaxes(
        lax.dynamic_slice_in_dim(rhs_blocks, core * half, half, 2), 1, 2
    ).reshape(node_total, planes, group, panel)
    own_group = sum(((plane >> b) & 1) << (levels - 2 - b) for b in range(levels - 1))
    columns = jnp.stack(
        [lax.dynamic_index_in_dim(flipped, own_group ^ g, 1, keepdims=False) for g in range(planes)],
        axis=1,
    )
    right_parts = []
    for o in range(planes):
        g = reverse(o)
        pieces = []
        for depth in range(levels - 1, -1, -1):
            node = first[depth] + ((plane ^ o) >> shift[depth])
            mine = pick(columns, node)
            for i in range(2**depth):
                pieces.append(mine[i ^ g])
        packed = jnp.concatenate(pieces, axis=0)
        right_parts.append(packed if o == 0 else move(packed, plane_mask=o))
    right = [None] * levels
    start = 0
    for depth in range(levels - 1, -1, -1):
        size = group * 2**depth
        right[depth] = jnp.concatenate([p[start : start + size] for p in right_parts], axis=1)
        start += size

    diag = [None] * levels
    lower = [None] * levels
    for depth in range(levels - 1, -1, -1):
        diag[depth] = pair_core(gather_node(diag_inverse, depth))
        if depth > 0:
            tagged = jnp.concatenate(
                [
                    lower_blocks[first[depth] : first[depth] + 2**depth],
                    jnp.pad(
                        update_rows[first[depth] : first[depth] + 2**depth, None, :].astype(jnp.float32),
                        ((0, 0), (0, 7), (0, piece - panel)),
                    ),
                ],
                axis=1,
            )
            parts = []
            for o in range(planes):
                block = pick(tagged, (plane ^ o) >> shift[depth])
                parts.append(block if o == 0 else move(block, plane_mask=o))
            own = jnp.stack(parts)
            both = jnp.concatenate([own, move(own, core_mask=1)], axis=2)
            body = both[:, :panel]
            names = both[:, panel, :panel]
            lower[depth] = []
            for up in range(depth):
                base = (first[up] + (plane >> shift[up])) * panel
                spots = (base + jnp.arange(panel, dtype=jnp.int32)).astype(jnp.float32)
                chosen = (names[:, None, :] == spots[None, :, None]).astype(jnp.float32)
                lower[depth].append(
                    jnp.einsum("otm,omr->otr", chosen, body, precision=lax.Precision.HIGHEST).reshape(
                        planes * panel, 2 * piece
                    )
                )

    forward = [None] * levels
    pending = [None] * levels
    work = right[levels - 1]
    for depth in range(levels - 1, -1, -1):
        forward[depth] = inner_sum(dot(work, diag[depth], ((1,), (0,))))
        if depth == 0:
            break
        keep = work.shape[0] // 2
        mask = 1 << shift[depth]
        for up in range(depth - 1, -1, -1):
            update = dot(forward[depth], lower[depth][up], ((1,), (1,)))
            if pending[up] is not None:
                update = update + pending[up]
            mine, theirs = update[:keep], reorder(update[keep:], mask)
            if up == depth - 1:
                work = right[up] - (cross_sum(mine) + cross_sum(theirs, mask))
            else:
                pending[up] = mine + move(theirs, plane_mask=mask)

    answer = [None] * levels
    for depth in range(levels):
        residual = forward[depth]
        if depth > 0:
            known = sum(dot(answer[up], lower[depth][up], ((1,), (0,))) for up in range(depth))
            residual = residual - inner_sum(known)
        partial_value = dot(residual, diag[depth], ((1,), (1,)))
        if depth < levels - 1:
            mask = 1 << shift[depth + 1]
            for up in range(depth):
                answer[up] = jnp.concatenate(
                    [answer[up], move(reorder(answer[up], mask), plane_mask=mask)], axis=0
                )
            answer[depth] = jnp.concatenate(
                [cross_sum(partial_value), cross_sum(reorder(partial_value, mask), mask)], axis=0
            )
        else:
            answer[depth] = cross_sum(partial_value)

    collected = [None] * node_total
    for depth in range(levels):
        for s in range(2**depth):
            o = s << shift[depth]
            block = answer[depth][:, o * panel : (o + 1) * panel]
            if o:
                block = move(regroup(block, o), plane_mask=o)
            collected[first[depth] + s] = block
    relative = jnp.stack(collected)
    other = move(relative, core_mask=1)
    both = jnp.where(core == 0, jnp.stack([relative, other]), jnp.stack([other, relative]))
    ordered = []
    for depth in range(levels - 1, -1, -1):
        for n in range(2**depth):
            node = first[depth] + (n ^ (plane >> shift[depth]))
            mine = lax.dynamic_index_in_dim(both, node, 1, keepdims=False).reshape(
                2, planes, group, panel
            )
            ordered.append(
                jnp.concatenate(
                    [lax.dynamic_index_in_dim(mine, own_group ^ g, 1, keepdims=False) for g in range(planes)],
                    axis=1,
                ).reshape(width, panel)
            )
    return jnp.swapaxes(jnp.stack(ordered), 1, 2)


def solution(mesh):
    placed = (
        P(None, "leaf", None),
        P(None, "leaf", "row"),
        P(None, "leaf", "row"),
        P(None, "leaf"),
    )
    return jax.shard_map(
        local, mesh=mesh, in_specs=placed, out_specs=P(None, "leaf", None), check_vma=False
    )
```

```python
import functools

import jax
import jax.numpy as jnp
from jax import lax
from jax.experimental import pallas as pl
from jax.experimental.pallas import tpu as pltpu
from jax.sharding import PartitionSpec as P

AXES = ("leaf", "row")
PRECISION = lax.Precision.HIGHEST


def dot(left, right, dims):
    return lax.dot_general(
        left, right, (dims, ((), ())), precision=PRECISION, preferred_element_type=jnp.float32
    )


def reverse(mask, bits):
    return sum(((mask >> b) & 1) << (bits - 1 - b) for b in range(bits))


def pack_kernel(levels, first, cross, spots, rhs, own, *rest):
    planes = 2 ** (levels - 1)
    messages, flat, lined = rest[: planes - 1], rest[-2], rest[-1]
    plane, core, across, own_group = spots[0], spots[1], spots[2], spots[3]
    panel = rhs.shape[1]
    half = rhs.shape[2] // 2
    group = half // planes
    columns = pl.ds(pl.multiple_of(core * half, half), half)
    slot = start = 0
    for depth in range(levels - 1, -1, -1):
        shift = levels - 1 - depth
        for s in range(2**depth):
            node = first[depth] + ((plane >> shift) ^ s)
            flat[slot] = rhs[node, :, columns].T
            for o in range(planes):
                if o >> shift != s:
                    continue
                for i in range(2**depth):
                    picked = own_group ^ (i ^ reverse(o, levels - 1))
                    lined[o, start + i * group : start + (i + 1) * group, :] = flat[
                        slot, pl.ds(pl.multiple_of(picked * group, group), group), :
                    ]
            slot += 1
        start += group * 2**depth
    own[...] = lined[0]
    part = lined.shape[1] // cross
    for o in range(1, planes):
        messages[o - 1][...] = lined[o, pl.ds(pl.multiple_of(across * part, 8), part), :]


def finish_kernel(levels, first, spots, *refs):
    total = 2**levels - 1
    planes = 2 ** (levels - 1)
    mine, theirs_upper, theirs_last, out, flat = refs[:total], refs[-4], refs[-3], refs[-2], refs[-1]
    plane, core, own_group = spots[0], spots[1], spots[3]
    half = out.shape[2] // 2
    group = half // planes
    slot = 0
    for depth in range(levels):
        shift = levels - 1 - depth
        for s in range(2**depth):
            node = first[depth] + ((plane >> shift) ^ s)
            index = 2**depth - 1 + s
            for side in range(2):
                for g in range(planes):
                    to = pl.ds(pl.multiple_of((own_group ^ g) * group, group), group)
                    rows = slice(g * group, (g + 1) * group)
                    if side == 0:
                        value = mine[index][rows, :]
                    elif depth < levels - 1:
                        value = theirs_upper[index, rows, :]
                    else:
                        value = theirs_last[s, rows, :]
                    flat[slot, to, :] = value
                place = core if side == 0 else 1 - core
                out[node, :, pl.ds(pl.multiple_of(place * half, half), half)] = flat[slot].T
                slot += 1


def after(value, *others):
    return lax.optimization_barrier((value,) + others)[0]


def local(rhs_blocks, diag_inverse, lower_blocks, update_rows):
    leaf_count = lax.axis_size("leaf")
    row_count = lax.axis_size("row")
    node_total, panel, width = rhs_blocks.shape
    piece = diag_inverse.shape[2]
    levels = (node_total + 1).bit_length() - 1
    bits = levels - 1
    planes = 2**bits
    inner = leaf_count // planes
    cross = row_count // 2
    half = width // 2
    group = half // planes
    first = [2**levels - 2 ** (d + 1) for d in range(levels)]
    shift = [levels - 1 - d for d in range(levels)]

    plane = lax.axis_index("leaf") // inner
    core = lax.axis_index("row") % 2
    across = lax.axis_index("row") // 2
    own_group = sum(((plane >> b) & 1) << (bits - 1 - b) for b in range(bits))
    spots = jnp.stack([plane, core, across, own_group]).astype(jnp.int32)

    def move(x, plane_mask=0, inner_mask=0, cross_mask=0, core_mask=0):
        pairs = []
        for leaf in range(leaf_count):
            for row in range(row_count):
                other_leaf = leaf ^ (plane_mask * inner + inner_mask)
                other_row = row ^ (cross_mask * 2 + core_mask)
                pairs.append((leaf * row_count + row, other_leaf * row_count + other_row))
        return lax.ppermute(x, AXES, pairs)

    def inner_sum(x):
        mask = 1
        while mask < inner:
            x = x + move(x, inner_mask=mask)
            mask *= 2
        return x

    def cross_sum(x, plane_mask=0):
        parts = [
            move(x, plane_mask=plane_mask, cross_mask=m) if m or plane_mask else x
            for m in range(cross)
        ]
        while len(parts) > 1:
            parts = [parts[i] + parts[i + 1] for i in range(0, len(parts), 2)]
        return parts[0]

    def reorder(x, mask):
        g = reverse(mask, bits)
        parts = [x[:, (p ^ g) * panel : ((p ^ g) + 1) * panel] for p in range(planes)]
        return jnp.concatenate(parts, axis=1)

    def regroup(x, mask):
        g = reverse(mask, bits)
        return jnp.concatenate(
            [x[(i ^ g) * group : ((i ^ g) + 1) * group] for i in range(planes)], axis=0
        )

    def pick(array, index):
        return lax.dynamic_index_in_dim(array, index, 0, keepdims=False)

    last = levels - 1
    diag_pieces = {0: pick(diag_inverse, first[last] + plane)}
    for o in range(1, planes):
        diag_pieces[o] = move(pick(diag_inverse, first[last] + (plane ^ o)), plane_mask=o)

    lines = sum(group * 2**d for d in range(levels))
    vmem = pl.BlockSpec(memory_space=pltpu.VMEM)
    packed = pl.pallas_call(
        functools.partial(pack_kernel, levels, first, cross),
        out_shape=[jax.ShapeDtypeStruct((lines, panel), jnp.float32)]
        + [jax.ShapeDtypeStruct((lines // cross, panel), jnp.float32)] * (planes - 1),
        in_specs=[pl.BlockSpec(memory_space=pltpu.SMEM), vmem],
        out_specs=[vmem] * planes,
        scratch_shapes=[
            pltpu.VMEM((node_total, half, panel), jnp.float32),
            pltpu.VMEM((planes, lines, panel), jnp.float32),
        ],
        name="pack",
    )(spots, rhs_blocks)
    arrived = jnp.stack([move(packed[o], plane_mask=o) for o in range(1, planes)])
    sides = [arrived] + [move(arrived, cross_mask=m) for m in range(1, cross)]
    part = lines // cross
    spread = jnp.concatenate(
        [sum(jnp.where(across ^ m == j, sides[m], 0.0) for m in range(cross)) for j in range(cross)],
        axis=1,
    )
    line_blocks = [packed[0]] + [spread[o - 1] for o in range(1, planes)]
    right = [None] * levels
    start = 0
    for depth in range(levels - 1, -1, -1):
        size = group * 2**depth
        right[depth] = jnp.concatenate(
            [line_blocks[reverse(p, bits)][start : start + size] for p in range(planes)], axis=1
        )
        start += size

    def in_order(parts):
        return jnp.concatenate([parts[reverse(p, bits)] for p in range(planes)], axis=0)

    def pair_core(own):
        return jnp.concatenate([own, move(own, core_mask=1)], axis=-1)

    diag = [None] * levels
    lower = [None] * levels
    diag[last] = pair_core(in_order(diag_pieces))

    def tagged(index):
        names = pick(update_rows, index).astype(jnp.float32)[None, :]
        return jnp.concatenate(
            [pick(lower_blocks, index), jnp.pad(names, ((0, 7), (0, piece - panel)))], axis=0
        )

    gate = diag_pieces[1]
    lower_pieces = {0: tagged(first[last] + plane)}
    for o in range(1, planes):
        lower_pieces[o] = move(after(tagged(first[last] + (plane ^ o)), gate), plane_mask=o)

    def spread_rows(body, names, depth, where):
        result = []
        for up in range(depth):
            base = (first[up] + (where >> shift[up])) * panel
            spot = (base + jnp.arange(panel, dtype=jnp.int32)).astype(jnp.float32)
            chosen = (names[..., None, :] == spot[:, None]).astype(jnp.float32)
            result.append(jnp.matmul(chosen, body, precision=lax.Precision.HIGHEST))
        return result

    both = pair_core(jnp.stack([lower_pieces[reverse(p, bits)] for p in range(planes)]))
    lower[last] = [
        block.reshape(planes * panel, 2 * piece)
        for block in spread_rows(both[:, :panel], both[:, panel, :panel], last, plane)
    ]

    def gather(blocks, depth):
        held = blocks[0]
        for s in range(1, 2**depth):
            held = jnp.concatenate([held, move(blocks[s], plane_mask=s << shift[depth])], axis=0)
        return held

    def spread_planes(held, depth):
        for b in range(shift[depth] - 1, -1, -1):
            held = jnp.concatenate([held, move(held, plane_mask=1 << b)], axis=0)
        return held

    gate = lower_pieces[1]
    for depth in range(last - 1, -1, -1):
        for kind in (0, 1):
            if kind and depth == 0:
                continue
            blocks = []
            for s in range(2**depth):
                node = first[depth] + ((plane >> shift[depth]) ^ s)
                if kind:
                    body = pick(lower_blocks, node)
                    names = pick(update_rows, node).astype(jnp.float32)
                    owner = ((plane >> shift[depth]) ^ s) << shift[depth]
                    body = jnp.concatenate(spread_rows(body, names, depth, owner), axis=0)
                else:
                    body = pick(diag_inverse, node)
                blocks.append(after(body, gate))
            held = spread_planes(gather(blocks, depth), depth)
            if kind == 0:
                diag[depth] = pair_core(held)
            else:
                wide = pair_core(held).reshape(planes, depth, panel, 2 * piece)
                lower[depth] = [
                    wide[:, up].reshape(planes * panel, 2 * piece) for up in range(depth)
                ]
            gate = held

    forward = [None] * levels
    pending = [None] * levels
    work = right[last]
    for depth in range(last, -1, -1):
        forward[depth] = inner_sum(dot(work, diag[depth], ((1,), (0,))))
        if depth == 0:
            break
        keep = work.shape[0] // 2
        mask = 1 << shift[depth]
        for up in range(depth - 1, -1, -1):
            update = dot(forward[depth], lower[depth][up], ((1,), (1,)))
            if pending[up] is not None:
                update = update + pending[up]
            mine, theirs = update[:keep], reorder(update[keep:], mask)
            if up == depth - 1:
                work = right[up] - (cross_sum(mine) + cross_sum(theirs, mask))
            else:
                pending[up] = mine + move(theirs, plane_mask=mask)

    answer = [None] * levels
    for depth in range(levels):
        residual = forward[depth]
        if depth > 0:
            known = sum(dot(answer[up], lower[depth][up], ((1,), (0,))) for up in range(depth))
            residual = residual - inner_sum(known)
        partial_value = dot(residual, diag[depth], ((1,), (1,)))
        if depth < last:
            mask = 1 << shift[depth + 1]
            for up in range(depth):
                answer[up] = jnp.concatenate(
                    [answer[up], move(reorder(answer[up], mask), plane_mask=mask)], axis=0
                )
            answer[depth] = jnp.concatenate(
                [cross_sum(partial_value), cross_sum(reorder(partial_value, mask), mask)], axis=0
            )
        else:
            answer[depth] = cross_sum(partial_value)

    collected = []
    for depth in range(levels):
        for s in range(2**depth):
            o = s << shift[depth]
            p = reverse(o, bits)
            block = answer[depth][:, p * panel : (p + 1) * panel]
            collected.append(move(regroup(block, o), plane_mask=o) if o else block)
    upper = move(jnp.stack(collected[: planes - 1]), core_mask=1)
    lowest = move(jnp.stack(collected[planes - 1 :]), core_mask=1)
    return pl.pallas_call(
        functools.partial(finish_kernel, levels, first),
        out_shape=jax.ShapeDtypeStruct(rhs_blocks.shape, jnp.float32),
        in_specs=[pl.BlockSpec(memory_space=pltpu.SMEM)] + [vmem] * (node_total + 2),
        out_specs=vmem,
        scratch_shapes=[pltpu.VMEM((2 * node_total, half, panel), jnp.float32)],
        name="finish",
    )(spots, *collected, upper, lowest)


def solution(mesh):
    placed = (
        P(None, "leaf", None),
        P(None, "leaf", "row"),
        P(None, "leaf", "row"),
        P(None, "leaf"),
    )
    return jax.shard_map(
        local, mesh=mesh, in_specs=placed, out_specs=P(None, "leaf", None), check_vma=False
    )
```

```python
import functools

import jax
import jax.numpy as jnp
from jax import lax
from jax.experimental import pallas as pl
from jax.experimental.pallas import tpu as pltpu
from jax.sharding import PartitionSpec as P

AXES = ("leaf", "row")
PRECISION = lax.Precision.HIGHEST


def dot(left, right, dims):
    return lax.dot_general(
        left, right, (dims, ((), ())), precision=PRECISION, preferred_element_type=jnp.float32
    )


def reverse(mask, bits):
    return sum(((mask >> b) & 1) << (bits - 1 - b) for b in range(bits))


def places(planes, inner):
    plane = lax.axis_index("leaf") // inner
    bits = planes.bit_length() - 1
    own_group = sum(((plane >> b) & 1) << (bits - 1 - b) for b in range(bits))
    row = lax.axis_index("row")
    return plane, row % 2, row // 2, own_group


def pack_kernel(levels, first, cross, inner, rhs, own, *rest):
    planes = 2 ** (levels - 1)
    messages, flat, lined = rest[: planes - 1], rest[-2], rest[-1]
    plane, core, across, own_group = places(planes, inner)
    panel = rhs.shape[1]
    half = rhs.shape[2] // 2
    group = half // planes
    columns = pl.ds(pl.multiple_of(core * half, half), half)
    slot = start = 0
    for depth in range(levels - 1, -1, -1):
        shift = levels - 1 - depth
        for s in range(2**depth):
            node = first[depth] + ((plane >> shift) ^ s)
            flat[slot] = rhs[node, :, columns].T
            for o in range(planes):
                if o >> shift != s:
                    continue
                for i in range(2**depth):
                    picked = own_group ^ (i ^ reverse(o, levels - 1))
                    lined[o, start + i * group : start + (i + 1) * group, :] = flat[
                        slot, pl.ds(pl.multiple_of(picked * group, group), group), :
                    ]
            slot += 1
        start += group * 2**depth
    own[...] = lined[0]
    part = lined.shape[1] // cross
    for o in range(1, planes):
        messages[o - 1][...] = lined[o, pl.ds(pl.multiple_of(across * part, 8), part), :]


def finish_kernel(levels, first, inner, *refs):
    total = 2**levels - 1
    planes = 2 ** (levels - 1)
    mine, theirs_upper, theirs_last, out, flat = refs[:total], refs[-4], refs[-3], refs[-2], refs[-1]
    plane, core, _, own_group = places(planes, inner)
    half = out.shape[2] // 2
    group = half // planes
    slot = 0
    for depth in range(levels):
        shift = levels - 1 - depth
        for s in range(2**depth):
            node = first[depth] + ((plane >> shift) ^ s)
            index = 2**depth - 1 + s
            for side in range(2):
                for g in range(planes):
                    to = pl.ds(pl.multiple_of((own_group ^ g) * group, group), group)
                    rows = slice(g * group, (g + 1) * group)
                    if side == 0:
                        value = mine[index][rows, :]
                    elif depth < levels - 1:
                        value = theirs_upper[index, rows, :]
                    else:
                        value = theirs_last[s, rows, :]
                    flat[slot, to, :] = value
                place = core if side == 0 else 1 - core
                out[node, :, pl.ds(pl.multiple_of(place * half, half), half)] = flat[slot].T
                slot += 1


def after(value, *others):
    return lax.optimization_barrier((value,) + others)[0]


def local(rhs_blocks, diag_inverse, lower_blocks, update_rows):
    leaf_count = lax.axis_size("leaf")
    row_count = lax.axis_size("row")
    node_total, panel, width = rhs_blocks.shape
    piece = diag_inverse.shape[2]
    levels = (node_total + 1).bit_length() - 1
    bits = levels - 1
    planes = 2**bits
    inner = leaf_count // planes
    cross = row_count // 2
    half = width // 2
    group = half // planes
    first = [2**levels - 2 ** (d + 1) for d in range(levels)]
    shift = [levels - 1 - d for d in range(levels)]

    plane = lax.axis_index("leaf") // inner
    across = lax.axis_index("row") // 2

    def move(x, plane_mask=0, inner_mask=0, cross_mask=0, core_mask=0):
        pairs = []
        for leaf in range(leaf_count):
            for row in range(row_count):
                other_leaf = leaf ^ (plane_mask * inner + inner_mask)
                other_row = row ^ (cross_mask * 2 + core_mask)
                pairs.append((leaf * row_count + row, other_leaf * row_count + other_row))
        return lax.ppermute(x, AXES, pairs)

    def inner_sum(x):
        mask = 1
        while mask < inner:
            x = x + move(x, inner_mask=mask)
            mask *= 2
        return x

    def cross_sum(x, plane_mask=0):
        parts = [
            move(x, plane_mask=plane_mask, cross_mask=m) if m or plane_mask else x
            for m in range(cross)
        ]
        while len(parts) > 1:
            parts = [parts[i] + parts[i + 1] for i in range(0, len(parts), 2)]
        return parts[0]

    def reorder(x, mask):
        g = reverse(mask, bits)
        parts = [x[:, (p ^ g) * panel : ((p ^ g) + 1) * panel] for p in range(planes)]
        return jnp.concatenate(parts, axis=1)

    def regroup(x, mask):
        g = reverse(mask, bits)
        return jnp.concatenate(
            [x[(i ^ g) * group : ((i ^ g) + 1) * group] for i in range(planes)], axis=0
        )

    def pick(array, index):
        return lax.dynamic_index_in_dim(array, index, 0, keepdims=False)

    last = levels - 1
    diag_pieces = {0: pick(diag_inverse, first[last] + plane)}
    for o in range(1, planes):
        diag_pieces[o] = move(pick(diag_inverse, first[last] + (plane ^ o)), plane_mask=o)

    lines = sum(group * 2**d for d in range(levels))
    vmem = pl.BlockSpec(memory_space=pltpu.VMEM)
    packed = pl.pallas_call(
        functools.partial(pack_kernel, levels, first, cross, inner),
        out_shape=[jax.ShapeDtypeStruct((lines, panel), jnp.float32)]
        + [jax.ShapeDtypeStruct((lines // cross, panel), jnp.float32)] * (planes - 1),
        in_specs=[vmem],
        out_specs=[vmem] * planes,
        scratch_shapes=[
            pltpu.VMEM((node_total, half, panel), jnp.float32),
            pltpu.VMEM((planes, lines, panel), jnp.float32),
        ],
        name="pack",
    )(rhs_blocks)
    arrived = jnp.stack([move(packed[o], plane_mask=o) for o in range(1, planes)])
    sides = [arrived] + [move(arrived, cross_mask=m) for m in range(1, cross)]
    part = lines // cross
    spread = jnp.concatenate(
        [sum(jnp.where(across ^ m == j, sides[m], 0.0) for m in range(cross)) for j in range(cross)],
        axis=1,
    )
    line_blocks = [packed[0]] + [spread[o - 1] for o in range(1, planes)]
    right = [None] * levels
    start = 0
    for depth in range(levels - 1, -1, -1):
        size = group * 2**depth
        right[depth] = jnp.concatenate(
            [line_blocks[reverse(p, bits)][start : start + size] for p in range(planes)], axis=1
        )
        start += size

    def in_order(parts):
        return jnp.concatenate([parts[reverse(p, bits)] for p in range(planes)], axis=0)

    def pair_core(own, count=4):
        parts = [move(part, core_mask=1) for part in jnp.split(own, count, axis=0)]
        return jnp.concatenate([own, jnp.concatenate(parts, axis=0)], axis=-1)

    diag = [None] * levels
    lower = [None] * levels
    diag[last] = pair_core(in_order(diag_pieces))

    def tagged(index):
        names = pick(update_rows, index).astype(jnp.float32)[None, :]
        return jnp.concatenate(
            [pick(lower_blocks, index), jnp.pad(names, ((0, 7), (0, piece - panel)))], axis=0
        )

    gate = diag_pieces[1]
    lower_pieces = {0: tagged(first[last] + plane)}
    for o in range(1, planes):
        lower_pieces[o] = move(after(tagged(first[last] + (plane ^ o)), gate), plane_mask=o)

    def spread_rows(body, names, depth, where):
        result = []
        for up in range(depth):
            base = (first[up] + (where >> shift[up])) * panel
            spot = (base + jnp.arange(panel, dtype=jnp.int32)).astype(jnp.float32)
            chosen = (names[..., None, :] == spot[:, None]).astype(jnp.float32)
            result.append(jnp.matmul(chosen, body, precision=lax.Precision.HIGHEST))
        return result

    both = pair_core(jnp.stack([lower_pieces[reverse(p, bits)] for p in range(planes)]))
    lower[last] = [
        block.reshape(planes * panel, 2 * piece)
        for block in spread_rows(both[:, :panel], both[:, panel, :panel], last, plane)
    ]

    def gather(blocks, depth):
        held = blocks[0]
        for s in range(1, 2**depth):
            held = jnp.concatenate([held, move(blocks[s], plane_mask=s << shift[depth])], axis=0)
        return held

    def spread_planes(held, depth):
        for b in range(shift[depth] - 1, -1, -1):
            held = jnp.concatenate([held, move(held, plane_mask=1 << b)], axis=0)
        return held

    def lower_block(depth, s):
        node = first[depth] + ((plane >> shift[depth]) ^ s)
        owner = ((plane >> shift[depth]) ^ s) << shift[depth]
        names = pick(update_rows, node).astype(jnp.float32)
        return jnp.concatenate(spread_rows(pick(lower_blocks, node), names, depth, owner), axis=0)

    def diag_block(depth, s):
        return pick(diag_inverse, first[depth] + ((plane >> shift[depth]) ^ s))

    gate = lower_pieces[2]
    far_diag = move(after(diag_block(1, 1), gate), plane_mask=2)
    held_diag = jnp.concatenate([diag_block(1, 0), far_diag], axis=0)
    near_diag = move(held_diag, plane_mask=1)
    diag[1] = pair_core(jnp.concatenate([held_diag, near_diag], axis=0), 4)
    far_mixed = move(after(jnp.concatenate([lower_block(1, 1), diag_block(0, 0)], axis=0), gate), plane_mask=2)
    held_lower = jnp.concatenate([lower_block(1, 0), far_mixed[:panel]], axis=0)
    held_zero = jnp.concatenate([diag_block(0, 0), far_mixed[panel:]], axis=0)
    near_mixed = move(jnp.concatenate([held_lower, held_zero], axis=0), plane_mask=1)
    lower[1] = [pair_core(jnp.concatenate([held_lower, near_mixed[: 2 * panel]], axis=0), 4)]
    diag[0] = pair_core(jnp.concatenate([held_zero, near_mixed[2 * panel :]], axis=0), 4)

    forward = [None] * levels
    pending = [None] * levels
    work = right[last]
    for depth in range(last, -1, -1):
        forward[depth] = inner_sum(dot(work, diag[depth], ((1,), (0,))))
        if depth == 0:
            break
        keep = work.shape[0] // 2
        mask = 1 << shift[depth]
        for up in range(depth - 1, -1, -1):
            update = dot(forward[depth], lower[depth][up], ((1,), (1,)))
            if pending[up] is not None:
                update = update + pending[up]
            mine, theirs = update[:keep], reorder(update[keep:], mask)
            if up == depth - 1:
                work = right[up] - (cross_sum(mine) + cross_sum(theirs, mask))
            else:
                pending[up] = mine + move(theirs, plane_mask=mask)

    answer = [None] * levels
    for depth in range(levels):
        residual = forward[depth]
        if depth > 0:
            known = sum(dot(answer[up], lower[depth][up], ((1,), (0,))) for up in range(depth))
            residual = residual - inner_sum(known)
        partial_value = dot(residual, diag[depth], ((1,), (1,)))
        if depth < last:
            mask = 1 << shift[depth + 1]
            for up in range(depth):
                answer[up] = jnp.concatenate(
                    [answer[up], move(reorder(answer[up], mask), plane_mask=mask)], axis=0
                )
            answer[depth] = jnp.concatenate(
                [cross_sum(partial_value), cross_sum(reorder(partial_value, mask), mask)], axis=0
            )
        else:
            answer[depth] = cross_sum(partial_value)

    collected = []
    for depth in range(levels):
        for s in range(2**depth):
            o = s << shift[depth]
            p = reverse(o, bits)
            block = answer[depth][:, p * panel : (p + 1) * panel]
            collected.append(move(regroup(block, o), plane_mask=o) if o else block)
    upper = move(jnp.stack(collected[: planes - 1]), core_mask=1)
    lowest = move(jnp.stack(collected[planes - 1 :]), core_mask=1)
    return pl.pallas_call(
        functools.partial(finish_kernel, levels, first, inner),
        out_shape=jax.ShapeDtypeStruct(rhs_blocks.shape, jnp.float32),
        in_specs=[vmem] * (node_total + 2),
        out_specs=vmem,
        scratch_shapes=[pltpu.VMEM((2 * node_total, half, panel), jnp.float32)],
        name="finish",
    )(*collected, upper, lowest)


def solution(mesh):
    placed = (
        P(None, "leaf", None),
        P(None, "leaf", "row"),
        P(None, "leaf", "row"),
        P(None, "leaf"),
    )
    return jax.shard_map(
        local, mesh=mesh, in_specs=placed, out_specs=P(None, "leaf", None), check_vma=False
    )
```

```python
import functools

import jax
import jax.numpy as jnp
from jax import lax
from jax.experimental import pallas as pl
from jax.experimental.pallas import tpu as pltpu
from jax.sharding import PartitionSpec as P

AXES = ("leaf", "row")
PRECISION = lax.Precision.HIGHEST


def dot(left, right, dims):
    return lax.dot_general(
        left, right, (dims, ((), ())), precision=PRECISION, preferred_element_type=jnp.float32
    )


def reverse(mask, bits):
    return sum(((mask >> b) & 1) << (bits - 1 - b) for b in range(bits))


def places(planes, inner):
    plane = lax.axis_index("leaf") // inner
    bits = planes.bit_length() - 1
    own_group = sum(((plane >> b) & 1) << (bits - 1 - b) for b in range(bits))
    row = lax.axis_index("row")
    return plane, row % 2, row // 2, own_group


def pack_kernel(levels, first, cross, inner, rhs, own, *rest):
    planes = 2 ** (levels - 1)
    messages, flat, lined = rest[: planes - 1], rest[-2], rest[-1]
    plane, core, across, own_group = places(planes, inner)
    panel = rhs.shape[1]
    half = rhs.shape[2] // 2
    group = half // planes
    columns = pl.ds(pl.multiple_of(core * half, half), half)
    slot = start = 0
    for depth in range(levels - 1, -1, -1):
        shift = levels - 1 - depth
        for s in range(2**depth):
            node = first[depth] + ((plane >> shift) ^ s)
            flat[slot] = rhs[node, :, columns].T
            for o in range(planes):
                if o >> shift != s:
                    continue
                for i in range(2**depth):
                    picked = own_group ^ (i ^ reverse(o, levels - 1))
                    lined[o, start + i * group : start + (i + 1) * group, :] = flat[
                        slot, pl.ds(pl.multiple_of(picked * group, group), group), :
                    ]
            slot += 1
        start += group * 2**depth
    own[...] = lined[0]
    part = lined.shape[1] // cross
    for o in range(1, planes):
        messages[o - 1][...] = lined[o, pl.ds(pl.multiple_of(across * part, 8), part), :]


def finish_kernel(levels, first, inner, *refs):
    total = 2**levels - 1
    planes = 2 ** (levels - 1)
    mine, theirs_upper, theirs_last, out, flat = refs[:total], refs[-4], refs[-3], refs[-2], refs[-1]
    plane, core, _, own_group = places(planes, inner)
    half = out.shape[2] // 2
    group = half // planes
    slot = 0
    for depth in range(levels):
        shift = levels - 1 - depth
        for s in range(2**depth):
            node = first[depth] + ((plane >> shift) ^ s)
            index = 2**depth - 1 + s
            for side in range(2):
                for g in range(planes):
                    to = pl.ds(pl.multiple_of((own_group ^ g) * group, group), group)
                    rows = slice(g * group, (g + 1) * group)
                    if side == 0:
                        value = mine[index][rows, :]
                    elif depth < levels - 1:
                        value = theirs_upper[index, rows, :]
                    else:
                        value = theirs_last[s, rows, :]
                    flat[slot, to, :] = value
                place = core if side == 0 else 1 - core
                out[node, :, pl.ds(pl.multiple_of(place * half, half), half)] = flat[slot].T
                slot += 1


def after(value, *others):
    return lax.optimization_barrier((value,) + others)[0]


def local(rhs_blocks, diag_inverse, lower_blocks, update_rows):
    leaf_count = lax.axis_size("leaf")
    row_count = lax.axis_size("row")
    node_total, panel, width = rhs_blocks.shape
    piece = diag_inverse.shape[2]
    levels = (node_total + 1).bit_length() - 1
    bits = levels - 1
    planes = 2**bits
    inner = leaf_count // planes
    cross = row_count // 2
    half = width // 2
    group = half // planes
    first = [2**levels - 2 ** (d + 1) for d in range(levels)]
    shift = [levels - 1 - d for d in range(levels)]

    plane = lax.axis_index("leaf") // inner
    across = lax.axis_index("row") // 2

    def move(x, plane_mask=0, inner_mask=0, cross_mask=0, core_mask=0):
        pairs = []
        for leaf in range(leaf_count):
            for row in range(row_count):
                other_leaf = leaf ^ (plane_mask * inner + inner_mask)
                other_row = row ^ (cross_mask * 2 + core_mask)
                pairs.append((leaf * row_count + row, other_leaf * row_count + other_row))
        return lax.ppermute(x, AXES, pairs)

    def inner_sum(x):
        mask = 1
        while mask < inner:
            x = x + move(x, inner_mask=mask)
            mask *= 2
        return x

    def cross_sum(x, plane_mask=0):
        parts = [
            move(x, plane_mask=plane_mask, cross_mask=m) if m or plane_mask else x
            for m in range(cross)
        ]
        while len(parts) > 1:
            parts = [parts[i] + parts[i + 1] for i in range(0, len(parts), 2)]
        return parts[0]

    def reorder(x, mask):
        g = reverse(mask, bits)
        parts = [x[:, (p ^ g) * panel : ((p ^ g) + 1) * panel] for p in range(planes)]
        return jnp.concatenate(parts, axis=1)

    def regroup(x, mask):
        g = reverse(mask, bits)
        return jnp.concatenate(
            [x[(i ^ g) * group : ((i ^ g) + 1) * group] for i in range(planes)], axis=0
        )

    def pick(array, index):
        return lax.dynamic_index_in_dim(array, index, 0, keepdims=False)

    last = levels - 1
    diag_pieces = {0: pick(diag_inverse, first[last] + plane)}
    for o in range(1, planes):
        diag_pieces[o] = move(pick(diag_inverse, first[last] + (plane ^ o)), plane_mask=o)

    lines = sum(group * 2**d for d in range(levels))
    vmem = pl.BlockSpec(memory_space=pltpu.VMEM)
    packed = pl.pallas_call(
        functools.partial(pack_kernel, levels, first, cross, inner),
        out_shape=[jax.ShapeDtypeStruct((lines, panel), jnp.float32)]
        + [jax.ShapeDtypeStruct((lines // cross, panel), jnp.float32)] * (planes - 1),
        in_specs=[vmem],
        out_specs=[vmem] * planes,
        scratch_shapes=[
            pltpu.VMEM((node_total, half, panel), jnp.float32),
            pltpu.VMEM((planes, lines, panel), jnp.float32),
        ],
        name="pack",
    )(rhs_blocks)
    arrived = jnp.stack([move(packed[o], plane_mask=o) for o in range(1, planes)])
    sides = [arrived] + [move(arrived, cross_mask=m) for m in range(1, cross)]
    part = lines // cross
    spread = jnp.concatenate(
        [sum(jnp.where(across ^ m == j, sides[m], 0.0) for m in range(cross)) for j in range(cross)],
        axis=1,
    )
    line_blocks = [packed[0]] + [spread[o - 1] for o in range(1, planes)]
    right = [None] * levels
    start = 0
    for depth in range(levels - 1, -1, -1):
        size = group * 2**depth
        right[depth] = jnp.concatenate(
            [line_blocks[reverse(p, bits)][start : start + size] for p in range(planes)], axis=1
        )
        start += size

    def in_order(parts):
        return jnp.concatenate([parts[reverse(p, bits)] for p in range(planes)], axis=0)

    def pair_core(own, count=4):
        parts = [move(part, core_mask=1) for part in jnp.split(own, count, axis=0)]
        return jnp.concatenate([own, jnp.concatenate(parts, axis=0)], axis=-1)

    diag = [None] * levels
    lower = [None] * levels
    diag[last] = pair_core(in_order(diag_pieces), 4)

    def tagged(index):
        names = pick(update_rows, index).astype(jnp.float32)[None, :]
        return jnp.concatenate(
            [pick(lower_blocks, index), jnp.pad(names, ((0, 7), (0, piece - panel)))], axis=0
        )

    gate = diag_pieces[1]
    lower_pieces = {0: tagged(first[last] + plane)}
    for o in range(1, planes):
        lower_pieces[o] = move(after(tagged(first[last] + (plane ^ o)), gate), plane_mask=o)

    def spread_rows(body, names, depth, where):
        result = []
        for up in range(depth):
            base = (first[up] + (where >> shift[up])) * panel
            spot = (base + jnp.arange(panel, dtype=jnp.int32)).astype(jnp.float32)
            chosen = (names[..., None, :] == spot[:, None]).astype(jnp.float32)
            result.append(jnp.matmul(chosen, body, precision=lax.Precision.HIGHEST))
        return result

    both = pair_core(jnp.stack([lower_pieces[reverse(p, bits)] for p in range(planes)]), 4)
    lower[last] = [
        block.reshape(planes * panel, 2 * piece)
        for block in spread_rows(both[:, :panel], both[:, panel, :panel], last, plane)
    ]

    def gather(blocks, depth):
        held = blocks[0]
        for s in range(1, 2**depth):
            held = jnp.concatenate([held, move(blocks[s], plane_mask=s << shift[depth])], axis=0)
        return held

    def spread_planes(held, depth):
        for b in range(shift[depth] - 1, -1, -1):
            held = jnp.concatenate([held, move(held, plane_mask=1 << b)], axis=0)
        return held

    def lower_block(depth, s):
        node = first[depth] + ((plane >> shift[depth]) ^ s)
        owner = ((plane >> shift[depth]) ^ s) << shift[depth]
        names = pick(update_rows, node).astype(jnp.float32)
        return jnp.concatenate(spread_rows(pick(lower_blocks, node), names, depth, owner), axis=0)

    def diag_block(depth, s):
        return pick(diag_inverse, first[depth] + ((plane >> shift[depth]) ^ s))

    gate = lower_pieces[2]
    far_diag = move(after(diag_block(1, 1), gate), plane_mask=2)
    held_diag = jnp.concatenate([diag_block(1, 0), far_diag], axis=0)
    near_diag = move(held_diag, plane_mask=1)
    diag[1] = pair_core(jnp.concatenate([held_diag, near_diag], axis=0), 1)
    far_mixed = move(after(jnp.concatenate([lower_block(1, 1), diag_block(0, 0)], axis=0), gate), plane_mask=2)
    held_lower = jnp.concatenate([lower_block(1, 0), far_mixed[:panel]], axis=0)
    held_zero = jnp.concatenate([diag_block(0, 0), far_mixed[panel:]], axis=0)
    near_mixed = move(jnp.concatenate([held_lower, held_zero], axis=0), plane_mask=1)
    lower[1] = [pair_core(jnp.concatenate([held_lower, near_mixed[: 2 * panel]], axis=0), 4)]
    diag[0] = pair_core(jnp.concatenate([held_zero, near_mixed[2 * panel :]], axis=0), 1)

    forward = [None] * levels
    pending = [None] * levels
    work = right[last]
    for depth in range(last, -1, -1):
        forward[depth] = inner_sum(dot(work, diag[depth], ((1,), (0,))))
        if depth == 0:
            break
        keep = work.shape[0] // 2
        mask = 1 << shift[depth]
        for up in range(depth - 1, -1, -1):
            update = dot(forward[depth], lower[depth][up], ((1,), (1,)))
            if pending[up] is not None:
                update = update + pending[up]
            mine, theirs = update[:keep], reorder(update[keep:], mask)
            if up == depth - 1:
                work = right[up] - (cross_sum(mine) + cross_sum(theirs, mask))
            else:
                pending[up] = mine + move(theirs, plane_mask=mask)

    answer = [None] * levels
    for depth in range(levels):
        residual = forward[depth]
        if depth > 0:
            known = sum(dot(answer[up], lower[depth][up], ((1,), (0,))) for up in range(depth))
            residual = residual - inner_sum(known)
        partial_value = dot(residual, diag[depth], ((1,), (1,)))
        if depth < last:
            mask = 1 << shift[depth + 1]
            for up in range(depth):
                answer[up] = jnp.concatenate(
                    [answer[up], move(reorder(answer[up], mask), plane_mask=mask)], axis=0
                )
            answer[depth] = jnp.concatenate(
                [cross_sum(partial_value), cross_sum(reorder(partial_value, mask), mask)], axis=0
            )
        else:
            answer[depth] = cross_sum(partial_value)

    collected = []
    for depth in range(levels):
        for s in range(2**depth):
            o = s << shift[depth]
            p = reverse(o, bits)
            block = answer[depth][:, p * panel : (p + 1) * panel]
            collected.append(move(regroup(block, o), plane_mask=o) if o else block)
    upper = move(jnp.stack(collected[: planes - 1]), core_mask=1)
    lowest = move(jnp.stack(collected[planes - 1 :]), core_mask=1)
    return pl.pallas_call(
        functools.partial(finish_kernel, levels, first, inner),
        out_shape=jax.ShapeDtypeStruct(rhs_blocks.shape, jnp.float32),
        in_specs=[vmem] * (node_total + 2),
        out_specs=vmem,
        scratch_shapes=[pltpu.VMEM((2 * node_total, half, panel), jnp.float32)],
        name="finish",
    )(*collected, upper, lowest)


def solution(mesh):
    placed = (
        P(None, "leaf", None),
        P(None, "leaf", "row"),
        P(None, "leaf", "row"),
        P(None, "leaf"),
    )
    return jax.shard_map(
        local, mesh=mesh, in_specs=placed, out_specs=P(None, "leaf", None), check_vma=False
    )
```

```python
import functools

import jax
import jax.numpy as jnp
from jax import lax
from jax.experimental import pallas as pl
from jax.experimental.pallas import tpu as pltpu
from jax.sharding import PartitionSpec as P

AXES = ("leaf", "row")
PRECISION = lax.Precision.HIGHEST


def dot(left, right, dims):
    return lax.dot_general(
        left, right, (dims, ((), ())), precision=PRECISION, preferred_element_type=jnp.float32
    )


def reverse(mask, bits):
    return sum(((mask >> b) & 1) << (bits - 1 - b) for b in range(bits))


def places(planes, inner):
    plane = lax.axis_index("leaf") // inner
    bits = planes.bit_length() - 1
    own_group = sum(((plane >> b) & 1) << (bits - 1 - b) for b in range(bits))
    row = lax.axis_index("row")
    return plane, row % 2, row // 2, own_group


def pack_kernel(levels, first, cross, inner, rhs, own, *rest):
    planes = 2 ** (levels - 1)
    messages, flat, lined = rest[: planes - 1], rest[-2], rest[-1]
    plane, core, across, own_group = places(planes, inner)
    panel = rhs.shape[1]
    half = rhs.shape[2] // 2
    group = half // planes
    columns = pl.ds(pl.multiple_of(core * half, half), half)
    slot = start = 0
    for depth in range(levels - 1, -1, -1):
        shift = levels - 1 - depth
        for s in range(2**depth):
            node = first[depth] + ((plane >> shift) ^ s)
            flat[slot] = rhs[node, :, columns].T
            for o in range(planes):
                if o >> shift != s:
                    continue
                for i in range(2**depth):
                    picked = own_group ^ (i ^ reverse(o, levels - 1))
                    lined[o, start + i * group : start + (i + 1) * group, :] = flat[
                        slot, pl.ds(pl.multiple_of(picked * group, group), group), :
                    ]
            slot += 1
        start += group * 2**depth
    own[...] = lined[0]
    part = lined.shape[1] // cross
    for o in range(1, planes):
        messages[o - 1][...] = lined[o, pl.ds(pl.multiple_of(across * part, 8), part), :]


def finish_kernel(levels, first, inner, *refs):
    total = 2**levels - 1
    planes = 2 ** (levels - 1)
    mine, theirs_upper, theirs_last, out, flat = refs[:total], refs[-4], refs[-3], refs[-2], refs[-1]
    plane, core, _, own_group = places(planes, inner)
    half = out.shape[2] // 2
    group = half // planes
    slot = 0
    for depth in range(levels):
        shift = levels - 1 - depth
        for s in range(2**depth):
            node = first[depth] + ((plane >> shift) ^ s)
            index = 2**depth - 1 + s
            for side in range(2):
                for g in range(planes):
                    to = pl.ds(pl.multiple_of((own_group ^ g) * group, group), group)
                    rows = slice(g * group, (g + 1) * group)
                    if side == 0:
                        value = mine[index][rows, :]
                    elif depth < levels - 1:
                        value = theirs_upper[index, rows, :]
                    else:
                        value = theirs_last[s, rows, :]
                    flat[slot, to, :] = value
                place = core if side == 0 else 1 - core
                out[node, :, pl.ds(pl.multiple_of(place * half, half), half)] = flat[slot].T
                slot += 1


def after(value, *others):
    return lax.optimization_barrier((value,) + others)[0]


def local(rhs_blocks, diag_inverse, lower_blocks, update_rows):
    leaf_count = lax.axis_size("leaf")
    row_count = lax.axis_size("row")
    node_total, panel, width = rhs_blocks.shape
    piece = diag_inverse.shape[2]
    levels = (node_total + 1).bit_length() - 1
    bits = levels - 1
    planes = 2**bits
    inner = leaf_count // planes
    cross = row_count // 2
    half = width // 2
    group = half // planes
    first = [2**levels - 2 ** (d + 1) for d in range(levels)]
    shift = [levels - 1 - d for d in range(levels)]

    plane = lax.axis_index("leaf") // inner
    across = lax.axis_index("row") // 2

    def move(x, plane_mask=0, inner_mask=0, cross_mask=0, core_mask=0):
        pairs = []
        for leaf in range(leaf_count):
            for row in range(row_count):
                other_leaf = leaf ^ (plane_mask * inner + inner_mask)
                other_row = row ^ (cross_mask * 2 + core_mask)
                pairs.append((leaf * row_count + row, other_leaf * row_count + other_row))
        return lax.ppermute(x, AXES, pairs)

    def inner_sum(x):
        mask = 1
        while mask < inner:
            x = x + move(x, inner_mask=mask)
            mask *= 2
        return x

    def cross_sum(x, plane_mask=0):
        parts = [
            move(x, plane_mask=plane_mask, cross_mask=m) if m or plane_mask else x
            for m in range(cross)
        ]
        while len(parts) > 1:
            parts = [parts[i] + parts[i + 1] for i in range(0, len(parts), 2)]
        return parts[0]

    def reorder(x, mask):
        g = reverse(mask, bits)
        parts = [x[:, (p ^ g) * panel : ((p ^ g) + 1) * panel] for p in range(planes)]
        return jnp.concatenate(parts, axis=1)

    def regroup(x, mask):
        g = reverse(mask, bits)
        return jnp.concatenate(
            [x[(i ^ g) * group : ((i ^ g) + 1) * group] for i in range(planes)], axis=0
        )

    def pick(array, index):
        return lax.dynamic_index_in_dim(array, index, 0, keepdims=False)

    last = levels - 1
    diag_pieces = {0: pick(diag_inverse, first[last] + plane)}
    for o in range(1, planes):
        diag_pieces[o] = move(pick(diag_inverse, first[last] + (plane ^ o)), plane_mask=o)

    lines = sum(group * 2**d for d in range(levels))
    vmem = pl.BlockSpec(memory_space=pltpu.VMEM)
    packed = pl.pallas_call(
        functools.partial(pack_kernel, levels, first, cross, inner),
        out_shape=[jax.ShapeDtypeStruct((lines, panel), jnp.float32)]
        + [jax.ShapeDtypeStruct((lines // cross, panel), jnp.float32)] * (planes - 1),
        in_specs=[vmem],
        out_specs=[vmem] * planes,
        scratch_shapes=[
            pltpu.VMEM((node_total, half, panel), jnp.float32),
            pltpu.VMEM((planes, lines, panel), jnp.float32),
        ],
        name="pack",
    )(rhs_blocks)
    arrived = jnp.stack([move(packed[o], plane_mask=o) for o in range(1, planes)])
    sides = [arrived] + [move(arrived, cross_mask=m) for m in range(1, cross)]
    part = lines // cross
    spread = jnp.concatenate(
        [sum(jnp.where(across ^ m == j, sides[m], 0.0) for m in range(cross)) for j in range(cross)],
        axis=1,
    )
    line_blocks = [packed[0]] + [spread[o - 1] for o in range(1, planes)]
    right = [None] * levels
    start = 0
    for depth in range(levels - 1, -1, -1):
        size = group * 2**depth
        right[depth] = jnp.concatenate(
            [line_blocks[reverse(p, bits)][start : start + size] for p in range(planes)], axis=1
        )
        start += size

    def in_order(parts):
        return jnp.concatenate([parts[reverse(p, bits)] for p in range(planes)], axis=0)

    def pair_core(own, count=4):
        parts = [move(part, core_mask=1) for part in jnp.split(own, count, axis=0)]
        return jnp.concatenate([own, jnp.concatenate(parts, axis=0)], axis=-1)

    diag = [None] * levels
    lower = [None] * levels
    diag[last] = pair_core(in_order(diag_pieces), 4)

    def tagged(index):
        names = pick(update_rows, index).astype(jnp.float32)[None, :]
        return jnp.concatenate(
            [pick(lower_blocks, index), jnp.pad(names, ((0, 7), (0, piece - panel)))], axis=0
        )

    gate = diag_pieces[3]
    lower_pieces = {0: tagged(first[last] + plane)}
    for o in range(1, planes):
        lower_pieces[o] = move(after(tagged(first[last] + (plane ^ o)), gate), plane_mask=o)

    def spread_rows(body, names, depth, where):
        result = []
        for up in range(depth):
            base = (first[up] + (where >> shift[up])) * panel
            spot = (base + jnp.arange(panel, dtype=jnp.int32)).astype(jnp.float32)
            chosen = (names[..., None, :] == spot[:, None]).astype(jnp.float32)
            result.append(jnp.matmul(chosen, body, precision=lax.Precision.HIGHEST))
        return result

    both = pair_core(jnp.stack([lower_pieces[reverse(p, bits)] for p in range(planes)]), 4)
    lower[last] = [
        block.reshape(planes * panel, 2 * piece)
        for block in spread_rows(both[:, :panel], both[:, panel, :panel], last, plane)
    ]

    def gather(blocks, depth):
        held = blocks[0]
        for s in range(1, 2**depth):
            held = jnp.concatenate([held, move(blocks[s], plane_mask=s << shift[depth])], axis=0)
        return held

    def spread_planes(held, depth):
        for b in range(shift[depth] - 1, -1, -1):
            held = jnp.concatenate([held, move(held, plane_mask=1 << b)], axis=0)
        return held

    def lower_block(depth, s):
        node = first[depth] + ((plane >> shift[depth]) ^ s)
        owner = ((plane >> shift[depth]) ^ s) << shift[depth]
        names = pick(update_rows, node).astype(jnp.float32)
        return jnp.concatenate(spread_rows(pick(lower_blocks, node), names, depth, owner), axis=0)

    def diag_block(depth, s):
        return pick(diag_inverse, first[depth] + ((plane >> shift[depth]) ^ s))

    gate = lower_pieces[3]
    far_diag = move(after(diag_block(1, 1), gate), plane_mask=2)
    held_diag = jnp.concatenate([diag_block(1, 0), far_diag], axis=0)
    near_diag = move(held_diag, plane_mask=1)
    diag[1] = pair_core(jnp.concatenate([held_diag, near_diag], axis=0), 1)
    far_mixed = move(after(jnp.concatenate([lower_block(1, 1), diag_block(0, 0)], axis=0), gate), plane_mask=2)
    held_lower = jnp.concatenate([lower_block(1, 0), far_mixed[:panel]], axis=0)
    held_zero = jnp.concatenate([diag_block(0, 0), far_mixed[panel:]], axis=0)
    near_mixed = move(jnp.concatenate([held_lower, held_zero], axis=0), plane_mask=1)
    lower[1] = [pair_core(jnp.concatenate([held_lower, near_mixed[: 2 * panel]], axis=0), 4)]
    diag[0] = pair_core(jnp.concatenate([held_zero, near_mixed[2 * panel :]], axis=0), 1)

    forward = [None] * levels
    pending = [None] * levels
    work = right[last]
    for depth in range(last, -1, -1):
        forward[depth] = inner_sum(dot(work, diag[depth], ((1,), (0,))))
        if depth == 0:
            break
        keep = work.shape[0] // 2
        mask = 1 << shift[depth]
        for up in range(depth - 1, -1, -1):
            update = dot(forward[depth], lower[depth][up], ((1,), (1,)))
            if pending[up] is not None:
                update = update + pending[up]
            mine, theirs = update[:keep], reorder(update[keep:], mask)
            if up == depth - 1:
                work = right[up] - (cross_sum(mine) + cross_sum(theirs, mask))
            else:
                pending[up] = mine + move(theirs, plane_mask=mask)

    answer = [None] * levels
    for depth in range(levels):
        residual = forward[depth]
        if depth > 0:
            known = sum(dot(answer[up], lower[depth][up], ((1,), (0,))) for up in range(depth))
            residual = residual - inner_sum(known)
        partial_value = dot(residual, diag[depth], ((1,), (1,)))
        if depth < last:
            mask = 1 << shift[depth + 1]
            for up in range(depth):
                answer[up] = jnp.concatenate(
                    [answer[up], move(reorder(answer[up], mask), plane_mask=mask)], axis=0
                )
            answer[depth] = jnp.concatenate(
                [cross_sum(partial_value), cross_sum(reorder(partial_value, mask), mask)], axis=0
            )
        else:
            answer[depth] = cross_sum(partial_value)

    collected = []
    for depth in range(levels):
        for s in range(2**depth):
            o = s << shift[depth]
            p = reverse(o, bits)
            block = answer[depth][:, p * panel : (p + 1) * panel]
            collected.append(move(regroup(block, o), plane_mask=o) if o else block)
    upper = move(jnp.stack(collected[: planes - 1]), core_mask=1)
    lowest = move(jnp.stack(collected[planes - 1 :]), core_mask=1)
    return pl.pallas_call(
        functools.partial(finish_kernel, levels, first, inner),
        out_shape=jax.ShapeDtypeStruct(rhs_blocks.shape, jnp.float32),
        in_specs=[vmem] * (node_total + 2),
        out_specs=vmem,
        scratch_shapes=[pltpu.VMEM((2 * node_total, half, panel), jnp.float32)],
        name="finish",
    )(*collected, upper, lowest)


def solution(mesh):
    placed = (
        P(None, "leaf", None),
        P(None, "leaf", "row"),
        P(None, "leaf", "row"),
        P(None, "leaf"),
    )
    return jax.shard_map(
        local, mesh=mesh, in_specs=placed, out_specs=P(None, "leaf", None), check_vma=False
    )
```

```python
import functools

import jax
import jax.numpy as jnp
from jax import lax
from jax.experimental import pallas as pl
from jax.experimental.pallas import tpu as pltpu
from jax.sharding import PartitionSpec as P

AXES = ("leaf", "row")
PRECISION = lax.Precision.HIGHEST


def dot(left, right, dims):
    return lax.dot_general(
        left, right, (dims, ((), ())), precision=PRECISION, preferred_element_type=jnp.float32
    )


def reverse(mask, bits):
    return sum(((mask >> b) & 1) << (bits - 1 - b) for b in range(bits))


def places(planes, inner):
    plane = lax.axis_index("leaf") // inner
    bits = planes.bit_length() - 1
    own_group = sum(((plane >> b) & 1) << (bits - 1 - b) for b in range(bits))
    row = lax.axis_index("row")
    return plane, row % 2, row // 2, own_group


def pack_kernel(levels, first, cross, inner, rhs, own, *rest):
    planes = 2 ** (levels - 1)
    messages, flat, lined = rest[: planes - 1], rest[-2], rest[-1]
    plane, core, across, own_group = places(planes, inner)
    panel = rhs.shape[1]
    half = rhs.shape[2] // 2
    group = half // planes
    columns = pl.ds(pl.multiple_of(core * half, half), half)
    slot = start = 0
    for depth in range(levels - 1, -1, -1):
        shift = levels - 1 - depth
        for s in range(2**depth):
            node = first[depth] + ((plane >> shift) ^ s)
            flat[slot] = rhs[node, :, columns].T
            for o in range(planes):
                if o >> shift != s:
                    continue
                for i in range(2**depth):
                    picked = own_group ^ (i ^ reverse(o, levels - 1))
                    lined[o, start + i * group : start + (i + 1) * group, :] = flat[
                        slot, pl.ds(pl.multiple_of(picked * group, group), group), :
                    ]
            slot += 1
        start += group * 2**depth
    own[...] = lined[0]
    part = lined.shape[1] // cross
    for o in range(1, planes):
        messages[o - 1][...] = lined[o, pl.ds(pl.multiple_of(across * part, 8), part), :]


def finish_kernel(levels, first, inner, *refs):
    total = 2**levels - 1
    planes = 2 ** (levels - 1)
    mine, theirs_upper, theirs_last, out, flat = refs[:total], refs[-4], refs[-3], refs[-2], refs[-1]
    plane, core, _, own_group = places(planes, inner)
    half = out.shape[2] // 2
    group = half // planes
    slot = 0
    for depth in range(levels):
        shift = levels - 1 - depth
        for s in range(2**depth):
            node = first[depth] + ((plane >> shift) ^ s)
            index = 2**depth - 1 + s
            for side in range(2):
                for g in range(planes):
                    to = pl.ds(pl.multiple_of((own_group ^ g) * group, group), group)
                    rows = slice(g * group, (g + 1) * group)
                    if side == 0:
                        value = mine[index][rows, :]
                    elif depth < levels - 1:
                        value = theirs_upper[index, rows, :]
                    else:
                        value = theirs_last[s, rows, :]
                    flat[slot, to, :] = value
                place = core if side == 0 else 1 - core
                out[node, :, pl.ds(pl.multiple_of(place * half, half), half)] = flat[slot].T
                slot += 1


def after(value, *others):
    return lax.optimization_barrier((value,) + others)[0]


def local(rhs_blocks, diag_inverse, lower_blocks, update_rows):
    leaf_count = lax.axis_size("leaf")
    row_count = lax.axis_size("row")
    node_total, panel, width = rhs_blocks.shape
    piece = diag_inverse.shape[2]
    levels = (node_total + 1).bit_length() - 1
    bits = levels - 1
    planes = 2**bits
    inner = leaf_count // planes
    cross = row_count // 2
    half = width // 2
    group = half // planes
    first = [2**levels - 2 ** (d + 1) for d in range(levels)]
    shift = [levels - 1 - d for d in range(levels)]

    plane = lax.axis_index("leaf") // inner
    across = lax.axis_index("row") // 2

    def move(x, plane_mask=0, inner_mask=0, cross_mask=0, core_mask=0):
        pairs = []
        for leaf in range(leaf_count):
            for row in range(row_count):
                other_leaf = leaf ^ (plane_mask * inner + inner_mask)
                other_row = row ^ (cross_mask * 2 + core_mask)
                pairs.append((leaf * row_count + row, other_leaf * row_count + other_row))
        return lax.ppermute(x, AXES, pairs)

    def inner_sum(x):
        mask = 1
        while mask < inner:
            x = x + move(x, inner_mask=mask)
            mask *= 2
        return x

    def cross_sum(x, plane_mask=0):
        parts = [
            move(x, plane_mask=plane_mask, cross_mask=m) if m or plane_mask else x
            for m in range(cross)
        ]
        while len(parts) > 1:
            parts = [parts[i] + parts[i + 1] for i in range(0, len(parts), 2)]
        return parts[0]

    def reorder(x, mask):
        g = reverse(mask, bits)
        parts = [x[:, (p ^ g) * panel : ((p ^ g) + 1) * panel] for p in range(planes)]
        return jnp.concatenate(parts, axis=1)

    def regroup(x, mask):
        g = reverse(mask, bits)
        return jnp.concatenate(
            [x[(i ^ g) * group : ((i ^ g) + 1) * group] for i in range(planes)], axis=0
        )

    def pick(array, index):
        return lax.dynamic_index_in_dim(array, index, 0, keepdims=False)

    last = levels - 1
    diag_pieces = {0: pick(diag_inverse, first[last] + plane)}
    for o in range(1, planes):
        diag_pieces[o] = move(pick(diag_inverse, first[last] + (plane ^ o)), plane_mask=o)

    lines = sum(group * 2**d for d in range(levels))
    vmem = pl.BlockSpec(memory_space=pltpu.VMEM)
    packed = pl.pallas_call(
        functools.partial(pack_kernel, levels, first, cross, inner),
        out_shape=[jax.ShapeDtypeStruct((lines, panel), jnp.float32)]
        + [jax.ShapeDtypeStruct((lines // cross, panel), jnp.float32)] * (planes - 1),
        in_specs=[vmem],
        out_specs=[vmem] * planes,
        scratch_shapes=[
            pltpu.VMEM((node_total, half, panel), jnp.float32),
            pltpu.VMEM((planes, lines, panel), jnp.float32),
        ],
        name="pack",
    )(rhs_blocks)
    arrived = jnp.stack([move(packed[o], plane_mask=o) for o in range(1, planes)])
    sides = [arrived] + [move(arrived, cross_mask=m) for m in range(1, cross)]
    part = lines // cross
    spread = jnp.concatenate(
        [sum(jnp.where(across ^ m == j, sides[m], 0.0) for m in range(cross)) for j in range(cross)],
        axis=1,
    )
    line_blocks = [packed[0]] + [spread[o - 1] for o in range(1, planes)]
    right = [None] * levels
    start = 0
    for depth in range(levels - 1, -1, -1):
        size = group * 2**depth
        right[depth] = jnp.concatenate(
            [line_blocks[reverse(p, bits)][start : start + size] for p in range(planes)], axis=1
        )
        start += size

    def in_order(parts):
        return jnp.concatenate([parts[reverse(p, bits)] for p in range(planes)], axis=0)

    def pair_core(own, count=4):
        parts = [move(part, core_mask=1) for part in jnp.split(own, count, axis=0)]
        return jnp.concatenate([own, jnp.concatenate(parts, axis=0)], axis=-1)

    diag = [None] * levels
    lower = [None] * levels
    diag[last] = pair_core(in_order(diag_pieces), 4)

    def tagged(index):
        names = pick(update_rows, index).astype(jnp.float32)[None, :]
        return jnp.concatenate(
            [pick(lower_blocks, index), jnp.pad(names, ((0, 7), (0, piece - panel)))], axis=0
        )

    gate = diag_pieces[2]
    lower_pieces = {0: tagged(first[last] + plane)}
    for o in range(1, planes):
        lower_pieces[o] = move(after(tagged(first[last] + (plane ^ o)), gate), plane_mask=o)

    def spread_rows(body, names, depth, where):
        result = []
        for up in range(depth):
            base = (first[up] + (where >> shift[up])) * panel
            spot = (base + jnp.arange(panel, dtype=jnp.int32)).astype(jnp.float32)
            chosen = (names[..., None, :] == spot[:, None]).astype(jnp.float32)
            result.append(jnp.matmul(chosen, body, precision=lax.Precision.HIGHEST))
        return result

    both = pair_core(jnp.stack([lower_pieces[reverse(p, bits)] for p in range(planes)]), 4)
    lower[last] = [
        block.reshape(planes * panel, 2 * piece)
        for block in spread_rows(both[:, :panel], both[:, panel, :panel], last, plane)
    ]

    def gather(blocks, depth):
        held = blocks[0]
        for s in range(1, 2**depth):
            held = jnp.concatenate([held, move(blocks[s], plane_mask=s << shift[depth])], axis=0)
        return held

    def spread_planes(held, depth):
        for b in range(shift[depth] - 1, -1, -1):
            held = jnp.concatenate([held, move(held, plane_mask=1 << b)], axis=0)
        return held

    def lower_block(depth, s):
        node = first[depth] + ((plane >> shift[depth]) ^ s)
        owner = ((plane >> shift[depth]) ^ s) << shift[depth]
        names = pick(update_rows, node).astype(jnp.float32)
        return jnp.concatenate(spread_rows(pick(lower_blocks, node), names, depth, owner), axis=0)

    def diag_block(depth, s):
        return pick(diag_inverse, first[depth] + ((plane >> shift[depth]) ^ s))

    gate = lower_pieces[3]
    far_diag = move(after(diag_block(1, 1), gate), plane_mask=2)
    held_diag = jnp.concatenate([diag_block(1, 0), far_diag], axis=0)
    near_diag = move(held_diag, plane_mask=1)
    diag[1] = pair_core(jnp.concatenate([held_diag, near_diag], axis=0), 1)
    far_mixed = move(after(jnp.concatenate([lower_block(1, 1), diag_block(0, 0)], axis=0), gate), plane_mask=2)
    held_lower = jnp.concatenate([lower_block(1, 0), far_mixed[:panel]], axis=0)
    held_zero = jnp.concatenate([diag_block(0, 0), far_mixed[panel:]], axis=0)
    near_mixed = move(jnp.concatenate([held_lower, held_zero], axis=0), plane_mask=1)
    lower[1] = [pair_core(jnp.concatenate([held_lower, near_mixed[: 2 * panel]], axis=0), 4)]
    diag[0] = pair_core(jnp.concatenate([held_zero, near_mixed[2 * panel :]], axis=0), 1)

    forward = [None] * levels
    pending = [None] * levels
    work = right[last]
    for depth in range(last, -1, -1):
        forward[depth] = inner_sum(dot(work, diag[depth], ((1,), (0,))))
        if depth == 0:
            break
        keep = work.shape[0] // 2
        mask = 1 << shift[depth]
        for up in range(depth - 1, -1, -1):
            update = dot(forward[depth], lower[depth][up], ((1,), (1,)))
            if pending[up] is not None:
                update = update + pending[up]
            mine, theirs = update[:keep], reorder(update[keep:], mask)
            if up == depth - 1:
                work = right[up] - (cross_sum(mine) + cross_sum(theirs, mask))
            else:
                pending[up] = mine + move(theirs, plane_mask=mask)

    answer = [None] * levels
    for depth in range(levels):
        residual = forward[depth]
        if depth > 0:
            known = sum(dot(answer[up], lower[depth][up], ((1,), (0,))) for up in range(depth))
            residual = residual - inner_sum(known)
        partial_value = dot(residual, diag[depth], ((1,), (1,)))
        if depth < last:
            mask = 1 << shift[depth + 1]
            for up in range(depth):
                answer[up] = jnp.concatenate(
                    [answer[up], move(reorder(answer[up], mask), plane_mask=mask)], axis=0
                )
            answer[depth] = jnp.concatenate(
                [cross_sum(partial_value), cross_sum(reorder(partial_value, mask), mask)], axis=0
            )
        else:
            answer[depth] = cross_sum(partial_value)

    collected = []
    for depth in range(levels):
        for s in range(2**depth):
            o = s << shift[depth]
            p = reverse(o, bits)
            block = answer[depth][:, p * panel : (p + 1) * panel]
            collected.append(move(regroup(block, o), plane_mask=o) if o else block)
    upper = move(jnp.stack(collected[: planes - 1]), core_mask=1)
    lowest = move(jnp.stack(collected[planes - 1 :]), core_mask=1)
    return pl.pallas_call(
        functools.partial(finish_kernel, levels, first, inner),
        out_shape=jax.ShapeDtypeStruct(rhs_blocks.shape, jnp.float32),
        in_specs=[vmem] * (node_total + 2),
        out_specs=vmem,
        scratch_shapes=[pltpu.VMEM((2 * node_total, half, panel), jnp.float32)],
        name="finish",
    )(*collected, upper, lowest)


def solution(mesh):
    placed = (
        P(None, "leaf", None),
        P(None, "leaf", "row"),
        P(None, "leaf", "row"),
        P(None, "leaf"),
    )
    return jax.shard_map(
        local, mesh=mesh, in_specs=placed, out_specs=P(None, "leaf", None), check_vma=False
    )
```
